32 devices in a mesh: az: 8 (over y, x, core), ax: 4 (over z).
Axes of the slice: x: 2, y: 2, z: 4, core: 2. Of those that a mesh axis runs over, the one named last changes fastest.
Arguments:
- step_start: float32 [5, 16, 512, 2048], P(None, None, 'ax', 'az'), may hold values from -3 to 12, as said below
- section_state: float32 [5, 16, 512, 2048], P(None, None, 'ax', 'az'), may hold values from -3 to 12, as said below
- near_rows: int32 [512], P('ax'), may hold values from 1 to 4
- cutoff: int32 [4, 512], P(None, 'ax'), may hold values from 64 to 511
- gore_map: int32 [512, 2048], P('ax', 'az'), may hold values from 0 to 80, as said below
Outputs:
- new_state: float32 [5, 16, 512, 2048], P(None, None, 'ax', 'az')
- gore_loads: float32 [80], replicated
The draws below stay inside these ranges and needn't reach their ends.
Inputs may be any that keep to these rules, and one draw needn't show every extreme that they name: `step_start`: every cell holds density, momentum and total energy of a gas state whose density and pressure lie between 0.5 and 2 and whose velocity components lie within 1.5 in magnitude. `section_state`: every cell holds density, momentum and total energy of a gas state whose density and pressure lie between 0.5 and 2 and whose velocity components lie within 1.5 in magnitude. `gore_map`: each axial station is either entirely gap, marked 80, or canopy whose gores run in azimuthal bands.
All inputs are finite; a program needn't handle non-finite values.
Results may differ from the reference program's by a relative error of at most 0.000077.
Values sent between devices are 32-bit elements; how exact they have to be, the bound alone decides.
A program may use at most 192 MiB of HBM per device.

```python
import math
import jax
import jax.numpy as jnp
from jax import lax

NA = 2048
NR = 16
NF = 4
GORES = 80
NX = 512


def flow_state(key):
    key_density, key_speed, key_pressure = jax.random.split(key, 3)
    grid_shape = (NR, NX, NA)
    density = jnp.exp(jax.random.uniform(key_density, grid_shape, jnp.float32, math.log(0.5), math.log(2.0)))
    velocity = jnp.clip(0.5 * jax.random.normal(key_speed, (3,) + grid_shape, jnp.float32), -1.5, 1.5)
    pressure = jnp.exp(jax.random.uniform(key_pressure, grid_shape, jnp.float32, math.log(0.5), math.log(2.0)))
    momentum = density[None] * velocity
    energy = pressure / 0.4 + 0.5 * density * jnp.sum(velocity * velocity, axis=0)
    return jnp.concatenate([density[None], momentum, energy[None]], axis=0)


def draw_step_start(key, part):
    return flow_state(jax.random.fold_in(key, 11))


def draw_section_state(key, part):
    return flow_state(jax.random.fold_in(key, 23))


def draw_gore_map(key, part):
    key_twist, key_gap = jax.random.split(jax.random.fold_in(key, 37))
    station = jnp.arange(NX, dtype=jnp.int32)[:, None]
    column = jnp.arange(NA, dtype=jnp.int32)[None, :]
    twist = jax.random.randint(key_twist, (NX, 1), 0, GORES)
    gap_rows = (jax.random.randint(key_gap, (NX, 1), 0, 4) == 0) | (station == NX // 2)
    owner = (column * GORES // NA + twist) % GORES
    return jnp.where(gap_rows, GORES, owner).astype(jnp.int32)


def with_ends(entries, rng, low, top_value):
    longest = entries.shape.index(max(entries.shape))
    spots = []
    for shift in (0, 1):
        where = [jax.random.randint(jax.random.fold_in(rng, axis), (), 0, length) for axis, length in enumerate(entries.shape)]
        where[longest] = (where[longest] + shift) % entries.shape[longest]
        spots.append(tuple(where))
    return entries.at[spots[0]].set(low).at[spots[1]].set(top_value)


def setup_inputs(seed: int = 0) -> dict:
    seeds = jax.random.split(jax.random.key(seed), 6)
    return {
        "step_start": draw_step_start(jax.random.fold_in(seeds[5], 71), 0),
        "section_state": draw_section_state(jax.random.fold_in(seeds[5], 71), 0),
        "near_rows": with_ends(jax.random.randint(seeds[2], (NX,), 1, NF + 1), jax.random.fold_in(seeds[2], 1), 1, NF).astype(jnp.int32),
        "cutoff": with_ends(jax.random.randint(seeds[3], (NF, NX), NA // 32, NA // 4), jax.random.fold_in(seeds[3], 1), NA // 32, (NA // 4) - 1).astype(jnp.int32),
        "gore_map": draw_gore_map(jax.random.fold_in(seeds[5], 71), 0),
    }


HEAT_RATIO = 1.4
WEIGHT_EPSILON = 1e-06
INNER_RADIUS = 24.0
RADIAL_STEP = 0.5
AXIAL_STEP = 0.5
TIME_STEP = 0.01
SECTION_KEEP = 1.0 / 3.0
SECTION_GAIN = 2.0 / 3.0

def slice_along(values, along_dim, start_at, length):
    return lax.slice_in_dim(values, start_at, start_at + length, axis=along_dim)

def pressure_of(conserved):
    density = conserved[0]
    kinetic = 0.5 * (conserved[1] * conserved[1] + conserved[2] * conserved[2] + conserved[3] * conserved[3]) / density
    return (HEAT_RATIO - 1.0) * (conserved[4] - kinetic)

def cell_fluxes(conserved, normal):
    density = conserved[0]
    velocity = conserved[normal] / density
    pressure = pressure_of(conserved)
    flux_parts = [conserved[0] * velocity, conserved[1] * velocity, conserved[2] * velocity, conserved[3] * velocity, (conserved[4] + pressure) * velocity]
    flux_parts[normal] = flux_parts[normal] + pressure
    wave_speed = jnp.abs(velocity) + jnp.sqrt(HEAT_RATIO * pressure / density)
    return (jnp.stack(flux_parts), wave_speed)

def weno_side(far_left, near_left, centre, near_right, far_right):
    cand_one = (2.0 * far_left - 7.0 * near_left + 11.0 * centre) / 6.0
    cand_two = (-near_left + 5.0 * centre + 2.0 * near_right) / 6.0
    cand_three = (2.0 * centre + 5.0 * near_right - far_right) / 6.0
    smooth_one = 13.0 / 12.0 * jnp.square(far_left - 2.0 * near_left + centre) + 0.25 * jnp.square(far_left - 4.0 * near_left + 3.0 * centre)
    smooth_two = 13.0 / 12.0 * jnp.square(near_left - 2.0 * centre + near_right) + 0.25 * jnp.square(near_left - near_right)
    smooth_three = 13.0 / 12.0 * jnp.square(centre - 2.0 * near_right + far_right) + 0.25 * jnp.square(3.0 * centre - 4.0 * near_right + far_right)
    weight_one = 0.1 / jnp.square(WEIGHT_EPSILON + smooth_one)
    weight_two = 0.6 / jnp.square(WEIGHT_EPSILON + smooth_two)
    weight_three = 0.3 / jnp.square(WEIGHT_EPSILON + smooth_three)
    weight_sum = weight_one + weight_two + weight_three
    return (weight_one * cand_one + weight_two * cand_two + weight_three * cand_three) / weight_sum

def face_fluxes(padded, along_dim, normal):
    face_count = padded.shape[along_dim] - 5
    flux_cells, wave_speed = cell_fluxes(padded, normal)
    damping = jnp.maximum(slice_along(wave_speed, along_dim - 1, 2, face_count), slice_along(wave_speed, along_dim - 1, 3, face_count))[None]

    def plus_part(offset):
        return 0.5 * (slice_along(flux_cells, along_dim, 2 + offset, face_count) + damping * slice_along(padded, along_dim, 2 + offset, face_count))

    def minus_part(offset):
        return 0.5 * (slice_along(flux_cells, along_dim, 2 + offset, face_count) - damping * slice_along(padded, along_dim, 2 + offset, face_count))
    return weno_side(plus_part(-2), plus_part(-1), plus_part(0), plus_part(1), plus_part(2)) + weno_side(minus_part(3), minus_part(2), minus_part(1), minus_part(0), minus_part(-1))

def cell_difference(face_values, along_dim):
    cell_count = face_values.shape[along_dim] - 1
    return slice_along(face_values, along_dim, 1, cell_count) - slice_along(face_values, along_dim, 0, cell_count)

def rate_of(cycle_padded, line_padded):
    interior = cycle_padded[:, :, :, 3:-3]
    row_count = interior.shape[1]
    radial_padded = jnp.pad(interior, ((0, 0), (3, 3), (0, 0), (0, 0)), mode='edge')
    face_radius = INNER_RADIUS + RADIAL_STEP * jnp.arange(row_count + 1, dtype=jnp.float32)
    cell_radius = INNER_RADIUS + RADIAL_STEP * (jnp.arange(row_count, dtype=jnp.float32) + 0.5)
    radial_faces = face_fluxes(radial_padded, 1, 1) * face_radius[None, :, None, None]
    radial_term = cell_difference(radial_faces, 1) / (RADIAL_STEP * cell_radius)[None, :, None, None]
    cycle_term = cell_difference(face_fluxes(cycle_padded, 3, 2), 3) / (cell_radius * (2.0 * math.pi / NA))[None, :, None, None]
    line_term = cell_difference(face_fluxes(line_padded, 2, 3), 2) / AXIAL_STEP
    pressure = pressure_of(interior)
    swirl_speed = interior[2] / interior[0]
    radius_cells = cell_radius[:, None, None]
    source_radial = (interior[2] * swirl_speed + pressure) / radius_cells
    source_swirl = -interior[1] * swirl_speed / radius_cells
    zero_field = jnp.zeros_like(pressure)
    sources = jnp.stack([zero_field, source_radial, source_swirl, zero_field, zero_field])
    return (interior, sources - radial_term - cycle_term - line_term)

def reference(step_start, section_state, near_rows, cutoff, gore_map):
    padded = jnp.pad(section_state, ((0, 0), (0, 0), (3, 3), (0, 0)), mode='edge')
    padded = jnp.pad(padded, ((0, 0), (0, 0), (0, 0), (3, 3)), mode='wrap')
    block_rows = 16
    block_count = NX // block_rows

    def one_block(block_index):
        first_row = block_index * block_rows
        slab_block = lax.dynamic_slice_in_dim(padded, first_row, block_rows + 6, axis=2)
        interior, tendency = rate_of(slab_block[:, :, 3:-3, :], slab_block[:, :, :, 3:-3])
        start_block = lax.dynamic_slice_in_dim(step_start, first_row, block_rows, axis=2)
        return SECTION_KEEP * start_block + SECTION_GAIN * (interior + TIME_STEP * tendency)
    blocks = lax.map(one_block, jnp.arange(block_count, dtype=jnp.int32))
    updated = jnp.moveaxis(blocks, 0, 2).reshape(5, NR, NX, NA)
    near_cycles = updated[:, :NF]
    spectrum = jnp.fft.rfft(near_cycles, axis=-1)
    mode_index = jnp.arange(NA // 2 + 1, dtype=jnp.int32)
    kept_modes = mode_index[None, None, :] < cutoff[:, :, None]
    smoothed = jnp.fft.irfft(jnp.where(kept_modes[None], spectrum, 0.0), n=NA, axis=-1)
    chosen = jnp.arange(NF, dtype=jnp.int32)[:, None] < near_rows[None, :]
    near_new = jnp.where(chosen[None, :, :, None], smoothed, near_cycles)
    new_state = jnp.concatenate([near_new, updated[:, NF:]], axis=1)
    canopy = NR // 2
    pressure_jump = pressure_of(section_state[:, canopy - 1]) - pressure_of(section_state[:, canopy + 1])
    axial_ramp = 1.0 + 2.0 * jnp.arange(NX, dtype=jnp.float32) / NX
    weighted = pressure_jump * axial_ramp[:, None] * (1.0 / math.sqrt(NX * NA / GORES))
    gore_loads = jax.ops.segment_sum(weighted.reshape(-1), gore_map.reshape(-1), num_segments=GORES + 1)[:GORES]
    return (new_state, gore_loads)
```

```python
import functools
import math

import jax
import jax.numpy as jnp
import numpy as np
from jax import lax
from jax.experimental import pallas as pl
from jax.experimental.pallas import tpu as pltpu
from jax.sharding import PartitionSpec as P

NA = 2048
NF = 4
GORES = 80

HEAT_RATIO = 1.4
WEIGHT_EPSILON = 1e-06
INNER_RADIUS = 24.0
RADIAL_STEP = 0.5
AXIAL_STEP = 0.5
TIME_STEP = 0.01
SECTION_KEEP = 1.0 / 3.0
SECTION_GAIN = 2.0 / 3.0

SB = 8
EPS = 3.0 * WEIGHT_EPSILON


def correction(d1, d2, d3, d4):
    e1 = d2 - d1
    e2 = d3 - d2
    e3 = d4 - d3
    h2 = 0.75 * d2
    h3 = 0.75 * d3
    s1 = (e1 * e1 + EPS) + h2 * (d2 + e1)
    s2 = (e2 * e2 + EPS) + h2 * d3
    s3 = (e3 * e3 + EPS) + h3 * (d3 - e3)
    y23 = s2 * s3
    y13 = s1 * s3
    y12 = s1 * s2
    a1 = y23 * y23
    a2 = y13 * y13
    a3 = 3.0 * (y12 * y12)
    den = a1 + 6.0 * a2 + a3
    num = (a1 + a1) * (e1 - e2) + a3 * (e2 - e3)
    return num * pl.reciprocal(den, approx=False)


def face_flux12(df, du, a, fsum):
    au = [a * x for x in du]
    pm2, pm1, p0, p1 = (df[k] + au[k] for k in range(4))
    mm1, m0, m1, m2 = (df[k] - au[k] for k in range(1, 5))
    cp = correction(pm2, pm1, p0, p1)
    cm = correction(m2, m1, m0, mm1)
    return 6.0 * fsum + ((pm1 - m1) - (au[2] + au[2]) + (cp - cm))


def primitives(u):
    rinv = 1.0 / u[0]
    kin = 0.5 * (u[1] * u[1] + u[2] * u[2] + u[3] * u[3]) * rinv
    p = (HEAT_RATIO - 1.0) * (u[4] - kin)
    cs = jnp.sqrt(HEAT_RATIO * p * rinv)
    return rinv, p, cs


def fluxes(u, vel, p, normal):
    f = [u[normal], u[1] * vel, u[2] * vel, u[3] * vel, (u[4] + p) * vel]
    f[normal] = f[normal] + p
    return f


def rk_kernel(cfg, *refs):
    r0, r1, q0, q1, rows_all, nblk, lt, has_alias = cfg
    state, lo, hi, left, right, start = refs[:6]
    out = refs[7] if has_alias else refs[6]
    U, FX, SX, RI, PR, CS, DR, SR, RF, CX, EX, sems = refs[8 if has_alias else 7:]
    nq = q1 - q0
    nr = r1 - r0
    st = nblk * SB
    i = pl.program_id(0)
    lane = lax.broadcasted_iota(jnp.int32, (lt, SB, 128), 2)
    lane1 = lax.broadcasted_iota(jnp.int32, (SB, 128), 1)
    sub = lax.broadcasted_iota(jnp.int32, (lt, SB, 128), 1)

    def axial_faces(c, q, base):
        def ld(ref, k, *ix):
            return ref[(*ix, q, slice(None), pl.ds(base + k, SB), slice(None))]

        uu = [ld(U, k, c) for k in range(-2, 4)]
        ff = [ld(U, k, 3) for k in range(-2, 4)] if c == 0 else [ld(FX, k, c - 1) for k in range(-2, 4)]
        a = jnp.maximum(ld(SX, 0), ld(SX, 1))
        df = [ff[k + 1] - ff[k] for k in range(5)]
        du = [uu[k + 1] - uu[k] for k in range(5)]
        return face_flux12(df, du, a, ff[2] + ff[3])

    @pl.when(i == 0)
    def _():
        copies = []
        for l in range(lt):
            ls = pl.ds(128 * l, 128)
            copies.append(pltpu.make_async_copy(
                state.at[:, pl.ds(q0, nq), :, ls], U.at[:, :, l, pl.ds(SB, st), :], sems.at[3 * l]))
            copies.append(pltpu.make_async_copy(
                lo.at[:, pl.ds(q0, nq), :, ls], U.at[:, :, l, pl.ds(0, SB), :], sems.at[3 * l + 1]))
            copies.append(pltpu.make_async_copy(
                hi.at[:, pl.ds(q0, nq), :, ls], U.at[:, :, l, pl.ds(SB + st, SB), :], sems.at[3 * l + 2]))
        for cp in copies:
            cp.start()
        for cp in copies:
            cp.wait()

        def close_end(at_end, to, end, edge):
            @pl.when(at_end)
            def _():
                def close_row(q, _):
                    for c in range(5):
                        cell = U[c, q, :, pl.ds(end, SB), :][:, edge:edge + 1]
                        U[c, q, :, pl.ds(to, SB), :] = jnp.broadcast_to(cell, (lt, SB, 128))
                    return 0

                lax.fori_loop(0, nq, close_row, 0)

        line = lax.axis_index("ax")
        close_end(line == 0, 0, SB, 0)
        close_end(line == lax.axis_size("ax") - 1, SB + st, st, SB - 1)

        def prim_row(q, _):
            def prim_block(b, _):
                ds = pl.ds(pl.multiple_of(b * SB, SB), SB)
                u = [U[c, q, :, ds, :] for c in range(5)]
                rinv, p, cs = primitives(u)
                vel = u[3] * rinv
                f = fluxes(u, vel, p, 3)
                for c in range(1, 5):
                    FX[c - 1, q, :, ds, :] = f[c]
                SX[q, :, ds, :] = jnp.abs(vel) + cs
                RI[q, :, ds, :] = rinv
                PR[q, :, ds, :] = p
                CS[q, :, ds, :] = cs
                return 0

            return lax.fori_loop(0, nblk + 2, prim_block, 0)

        lax.fori_loop(0, nq, prim_row, 0)

        def first_faces(r, _):
            for c in range(5):
                f = axial_faces(c, r + (r0 - q0), SB - 4)
                CX[c, r] = pltpu.roll(f, 4, 1)
            return 0

        lax.fori_loop(0, nr, first_faces, 0)

    base = pl.multiple_of(i * SB + SB, SB)
    ds = pl.ds(base, SB)

    hs = pl.ds(pl.multiple_of(i * SB, SB), SB)
    u = [left[c, hs, :] for c in range(5)]
    rinv, p, cs = primitives(u)
    vel = u[2] * rinv
    f = fluxes(u, vel, p, 2)
    s = jnp.abs(vel) + cs
    a = jnp.maximum(s, pltpu.roll(s, 127, 1))
    for c in range(5):
        df0 = pltpu.roll(f[c], 127, 1) - f[c]
        du0 = pltpu.roll(u[c], 127, 1) - u[c]
        df = [df0 if k == 0 else pltpu.roll(df0, (-k) % 128, 1) for k in range(-2, 3)]
        du = [du0 if k == 0 else pltpu.roll(du0, (-k) % 128, 1) for k in range(-2, 3)]
        EX[c] = face_flux12(df, du, a, f[c] + pltpu.roll(f[c], 127, 1))

    def radial_flux(q):
        u = [U[c, q, :, ds, :] for c in range(5)]
        vel = u[1] * RI[q, :, ds, :]
        f = fluxes(u, vel, PR[q, :, ds, :], 1)
        return u, f, jnp.abs(vel) + CS[q, :, ds, :]

    ne = nr + 5

    def radial_edge(e, carry):
        u, f = carry[:5], carry[5:10]
        q = jnp.clip(e + (r0 - 3) + 1, 0, rows_all - 1) - q0
        un, fn, sn = radial_flux(q)
        for c in range(5):
            DR[c, 0, e] = fn[c] - f[c]
            DR[c, 1, e] = un[c] - u[c]
            RF[c, e] = fn[c] + f[c]
        SR[e] = jnp.maximum(carry[10], sn)
        return (*un, *fn, sn)

    u, f, s = radial_flux(max(r0 - 3, 0) - q0)
    lax.fori_loop(0, ne, radial_edge, (*u, *f, s))

    def radial_face(c, e):
        df = [DR[c, 0, e + k] for k in range(-2, 3)]
        du = [DR[c, 1, e + k] for k in range(-2, 3)]
        return face_flux12(df, du, SR[e], RF[c, e])

    gain = SECTION_GAIN * TIME_STEP

    def one_row(r, low_faces):
        q = r + (r0 - q0)
        row = (r + r0).astype(jnp.float32)
        radius = INNER_RADIUS + RADIAL_STEP * (row + 0.5)
        rr = 1.0 / jnp.full((1, 1, 128), radius, jnp.float32)
        k_low = (gain / 12.0 / RADIAL_STEP) * (INNER_RADIUS + RADIAL_STEP * row) * rr
        k_up = (gain / 12.0 / RADIAL_STEP) * (INNER_RADIUS + RADIAL_STEP * (row + 1.0)) * rr
        k_cycle = (gain / 12.0 * NA / (2.0 * math.pi)) * rr
        k_line = gain / 12.0 / AXIAL_STEP
        k_src = gain * rr
        lr = r + r0
        uc = []
        for c in range(5):
            halo = jnp.where(
                lane1 < 64,
                pltpu.roll(right[c, hs, :], 125 - 8 * lr, 1),
                pltpu.roll(left[c, hs, :], 125 - 8 * lr, 1),
            )
            uc.append(jnp.concatenate([U[c, q, :, ds, :], halo[None]], axis=0))
        hr, hp, hc = primitives([x[lt:] for x in uc])
        rinv = jnp.concatenate([RI[q, :, ds, :], hr], axis=0)
        p = jnp.concatenate([PR[q, :, ds, :], hp], axis=0)
        cs = jnp.concatenate([CS[q, :, ds, :], hc], axis=0)
        vel = uc[2] * rinv
        fc = fluxes(uc, vel, p, 2)
        s = jnp.abs(vel) + cs

        def sh(x, k):
            if k == 0:
                return x[:lt]
            y = pltpu.roll(x, (-k) % 128, 2)
            if k > 0:
                return jnp.where(lane >= 128 - k, y[1:], y[:lt])
            prev = jnp.concatenate([y[lt:], y[:lt - 1]], axis=0) if lt > 1 else y[lt:]
            return jnp.where(lane < -k, prev, y[:lt])

        a_cycle = jnp.maximum(s[:lt], sh(s, 1))
        v0 = vel[:lt]
        src = {
            1: k_src * (uc[2][:lt] * v0 + p[:lt]),
            2: -k_src * (uc[1][:lt] * v0),
        }
        ups = []
        for c in range(5):
            up = radial_face(c, r + 3)
            ups.append(up)
            delta = k_low * low_faces[c] - k_up * up
            ff = [sh(fc[c], k) for k in range(-2, 4)]
            uu = [sh(uc[c], k) for k in range(-2, 4)]
            df = [ff[k + 1] - ff[k] for k in range(5)]
            du = [uu[k + 1] - uu[k] for k in range(5)]
            fa = face_flux12(df, du, a_cycle, ff[2] + ff[3])
            fa1 = pltpu.roll(fa, 1, 2)
            ex = pltpu.roll(EX[c], 126 - 8 * lr, 1)[None]
            prev = jnp.concatenate([ex, fa1[:lt - 1]], axis=0) if lt > 1 else ex
            delta = delta - k_cycle * (fa - jnp.where(lane == 0, prev, fa1))
            fx = axial_faces(c, q, base)
            before = jnp.where(sub == 0, pltpu.roll(CX[c, r], 1, 1), pltpu.roll(fx, 1, 1))
            CX[c, r] = fx
            delta = delta - k_line * (fx - before)
            if c in src:
                delta = delta + src[c]
            delta = delta + SECTION_GAIN * uc[c][:lt]
            for l in range(lt):
                ls = slice(128 * l, 128 * l + 128)
                out[c, r, :, ls] = SECTION_KEEP * start[c, r, :, ls] + delta[l]
        return tuple(ups)

    lax.fori_loop(0, nr, one_row, tuple(radial_face(c, 2) for c in range(5)))


def rk_rows(state, lo, hi, left, right, start, r0, r1, share=None, into=None):
    _, rows, stations, cells = state.shape
    lt = cells // 128
    nblk = stations // SB
    q0, q1 = max(r0 - 3, 0), min(r1 + 3, rows)
    nq, nr = q1 - q0, r1 - r0
    whole = into is not None
    cfg = (r0, r1, q0, q1, rows, nblk, lt, whole and into is not False)
    any_spec = pl.BlockSpec(memory_space=pl.ANY)
    halo_spec = pl.BlockSpec((5, stations, 128), lambda i: (0, 0, 0))
    step = r0 // nr
    in_specs = [any_spec, any_spec, any_spec, halo_spec, halo_spec,
                pl.BlockSpec((5, nr, SB, cells), lambda i: (0, step, i, 0))]
    args = [state, lo, hi, left, right, start]
    alias = {}
    if cfg[-1]:
        in_specs.append(any_spec)
        args.append(into)
        alias = {6: 0}
    if whole:
        out_shape = (5, rows, stations, cells)
        out_spec = pl.BlockSpec((5, nr, SB, cells), lambda i: (0, step, i, 0))
    else:
        group = share // SB
        out_shape = (stations // share, 5, nr, share, cells)
        out_spec = pl.BlockSpec(
            (None, 5, nr, SB, cells), lambda i: (i // group, 0, 0, i % group, 0))
    sp = stations + 2 * SB
    f32 = jnp.float32
    field = pltpu.VMEM((nq, lt, sp, 128), f32)
    return pl.pallas_call(
        functools.partial(rk_kernel, cfg),
        out_shape=jax.ShapeDtypeStruct(out_shape, f32),
        grid=(nblk,),
        in_specs=in_specs,
        out_specs=out_spec,
        scratch_shapes=[
            pltpu.VMEM((5, nq, lt, sp, 128), f32),
            pltpu.VMEM((4, nq, lt, sp, 128), f32),
            field, field, field, field,
            pltpu.VMEM((5, 2, nr + 5, lt, SB, 128), f32),
            pltpu.VMEM((nr + 5, lt, SB, 128), f32),
            pltpu.VMEM((5, nr + 5, lt, SB, 128), f32),
            pltpu.VMEM((5, nr, lt, SB, 128), f32),
            pltpu.VMEM((5, SB, 128), f32),
            pltpu.SemaphoreType.DMA((3 * lt,)),
        ],
        input_output_aliases=alias,
        compiler_params=pltpu.CompilerParams(
            dimension_semantics=("arbitrary",), vmem_limit_bytes=56 << 20),
        name="rk_rows_%d_%d" % (r0, r1),
    )(*args)


def merge_kernel(near, smooth, rows_ref, whole, out):
    for j in range(NF):
        keep = j < rows_ref[...]
        for c in range(5):
            out[c, j] = jnp.where(keep, smooth[c, j], near[c, j])


def merge_near(near, smooth, near_rows, whole):
    groups, _, _, share, cells = near.shape
    spec = pl.BlockSpec((None, 5, NF, share, cells), lambda i: (i, 0, 0, 0, 0))
    return pl.pallas_call(
        merge_kernel,
        out_shape=jax.ShapeDtypeStruct(whole.shape, jnp.float32),
        grid=(groups,),
        in_specs=[spec, spec, pl.BlockSpec((share, 1), lambda i: (i, 0)),
                  pl.BlockSpec(memory_space=pl.ANY)],
        out_specs=pl.BlockSpec((5, NF, share, cells), lambda i: (0, 0, i, 0)),
        input_output_aliases={3: 0},
        name="merge_near",
    )(near, smooth, near_rows[:, None], whole)


def edge_kernel(head, tail, out):
    rows = head.shape[1]
    lane = lax.broadcasted_iota(jnp.int32, head.shape[2:], 1)
    for c in range(5):
        acc = jnp.zeros(head.shape[2:], jnp.float32)
        for r in range(rows):
            ends = jnp.where(lane < 64, head[c, r], tail[c, r])
            ends = pltpu.roll(ends, (8 * r + 3) % 128, 1)
            acc = jnp.where((lane >= 8 * r) & (lane < 8 * r + 8), ends, acc)
        out[c] = acc


def azimuthal_edges(state):
    _, rows, stations, cells = state.shape
    sb = 32
    far = cells // 128 - 1
    return pl.pallas_call(
        edge_kernel,
        out_shape=jax.ShapeDtypeStruct((5, stations, rows * 8), jnp.float32),
        grid=(stations // sb,),
        in_specs=[pl.BlockSpec((5, rows, sb, 128), lambda i: (0, 0, i, 0)),
                  pl.BlockSpec((5, rows, sb, 128), lambda i: (0, 0, i, far))],
        out_specs=pl.BlockSpec((5, sb, rows * 8), lambda i: (0, i, 0)),
        name="azimuthal_edges",
    )(state, state)


def mode_tables():
    n = np.arange(NA // 2)[:, None]
    tables = []
    for parity in (0, 1):
        k = np.arange(parity, NA // 4, 2)[None, :]
        angle = 2.0 * math.pi / NA * ((n * k) % NA)
        tables.append(np.concatenate([np.cos(angle), np.sin(angle)], axis=1).astype(np.float32))
    return tables


def low_pass(cycles, cutoffs):
    half = NA // 2
    pieces, shape = cycles.shape[0], cycles.shape[1:]
    x = jnp.transpose(cycles, (1, 2, 3, 0, 4)).reshape(-1, NA)
    parts = (x[:, :half] + x[:, half:], x[:, :half] - x[:, half:])
    back = []
    for parity, table in enumerate(mode_tables()):
        k = np.arange(parity, NA // 4, 2)
        weight = np.where(k == 0, 1.0 / NA, 2.0 / NA).astype(np.float32)
        k2 = jnp.asarray(np.concatenate([k, k]).astype(np.int32))
        w2 = jnp.asarray(np.concatenate([weight, weight]))
        basis = jnp.asarray(table)
        coef = jnp.einsum("rn,nc->rc", parts[parity], basis, precision=lax.Precision.HIGH)
        gains = jnp.where(k2 < cutoffs[..., None], w2, 0.0)
        coef = (coef.reshape(shape[:3] + (-1,)) * gains[None]).reshape(x.shape[0], -1)
        back.append(jnp.einsum("rc,nc->rn", coef, basis, precision=lax.Precision.HIGH))
    y = jnp.concatenate([back[0] + back[1], back[0] - back[1]], axis=1)
    return jnp.transpose(y.reshape(shape[:3] + (pieces, -1)), (3, 0, 1, 2, 4))


def pressure_of(conserved):
    density = conserved[0]
    kinetic = (
        0.5
        * (conserved[1] * conserved[1] + conserved[2] * conserved[2] + conserved[3] * conserved[3])
        / density
    )
    return (HEAT_RATIO - 1.0) * (conserved[4] - kinetic)


def per_device(step_start, section_state, near_rows, cutoff, gore_map):
    _, rows, stations, cells = section_state.shape
    na, nx = lax.axis_size("az"), lax.axis_size("ax")
    cycle_index, line_index = lax.axis_index("az"), lax.axis_index("ax")
    up_a = [(i, (i + 1) % na) for i in range(na)]
    down_a = [((i + 1) % na, i) for i in range(na)]
    up_x = [(i, (i + 1) % nx) for i in range(nx)]
    down_x = [((i + 1) % nx, i) for i in range(nx)]

    edges = azimuthal_edges(section_state)
    from_left = lax.ppermute(edges, "az", up_a)
    right = lax.ppermute(edges, "az", down_a)
    lanes = jnp.arange(rows * 8, dtype=jnp.int32) % 8
    left = jnp.where(lanes < 3, from_left, edges)

    lo = lax.ppermute(section_state[:, :, -3:], "ax", up_x)
    hi = lax.ppermute(section_state[:, :, :3], "ax", down_x)
    lo = jnp.pad(lo, ((0, 0), (0, 0), (SB - 3, 0), (0, 0)), constant_values=1.0)
    hi = jnp.pad(hi, ((0, 0), (0, 0), (0, SB - 3), (0, 0)), constant_values=1.0)

    rest = functools.partial(rk_rows, section_state, lo, hi, left, right, step_start)
    share = stations // na
    near = rest(0, NF, share=share)
    spread = lax.all_to_all(near, "az", 0, 0, tiled=True)
    whole = rest(NF, 2 * NF, into=False)
    spread, whole = lax.optimization_barrier((spread, whole))
    cutoffs = lax.dynamic_slice_in_dim(cutoff, cycle_index * share, share, axis=1)
    kept = low_pass(spread, cutoffs)
    kept, whole = lax.optimization_barrier((kept, whole))
    smooth = lax.all_to_all(kept, "az", 0, 0, tiled=True)
    whole = rest(2 * NF, rows, into=whole)

    canopy = rows // 2
    jump = pressure_of(section_state[:, canopy - 1]) - pressure_of(section_state[:, canopy + 1])
    total = stations * nx
    station = line_index * stations + jnp.arange(stations, dtype=jnp.int32)
    ramp = 1.0 + 2.0 * station.astype(jnp.float32) / total
    weighted = jump * ramp[:, None] * (1.0 / math.sqrt(total * NA / GORES))
    gores = jnp.arange(GORES, dtype=jnp.int32)
    partial = jnp.sum(
        jnp.where(gore_map[None] == gores[:, None, None], weighted[None], 0.0), axis=(1, 2))
    partial, whole = lax.optimization_barrier((partial, whole))
    new_state = merge_near(near, smooth, near_rows, whole)
    gore_loads = lax.psum(partial, ("az", "ax"))
    return (new_state, gore_loads)


def solution(mesh):
    in_specs = (
        P(None, None, "ax", "az"),
        P(None, None, "ax", "az"),
        P("ax"),
        P(None, "ax"),
        P("ax", "az"),
    )
    out_specs = (P(None, None, "ax", "az"), P())
    return jax.shard_map(
        per_device, mesh=mesh, in_specs=in_specs, out_specs=out_specs, check_vma=False
    )
```

```python
import functools
import math

import jax
import jax.numpy as jnp
import numpy as np
from jax import lax
from jax.experimental import pallas as pl
from jax.experimental.pallas import tpu as pltpu
from jax.sharding import PartitionSpec as P

NA = 2048
NF = 4
GORES = 80

HEAT_RATIO = 1.4
WEIGHT_EPSILON = 1e-06
INNER_RADIUS = 24.0
RADIAL_STEP = 0.5
AXIAL_STEP = 0.5
TIME_STEP = 0.01
SECTION_KEEP = 1.0 / 3.0
SECTION_GAIN = 2.0 / 3.0

SB = 8
EPS = 3.0 * WEIGHT_EPSILON


def correction(d1, d2, d3, d4):
    e1 = d2 - d1
    e2 = d3 - d2
    e3 = d4 - d3
    h2 = 0.75 * d2
    h3 = 0.75 * d3
    s1 = (e1 * e1 + EPS) + h2 * (d2 + e1)
    s2 = (e2 * e2 + EPS) + h2 * d3
    s3 = (e3 * e3 + EPS) + h3 * (d3 - e3)
    y23 = s2 * s3
    y13 = s1 * s3
    y12 = s1 * s2
    a1 = y23 * y23
    a2 = y13 * y13
    a3 = 3.0 * (y12 * y12)
    den = a1 + 6.0 * a2 + a3
    num = (a1 + a1) * (e1 - e2) + a3 * (e2 - e3)
    return num * pl.reciprocal(den, approx=False)


def face_flux12(df, du, a, fsum):
    au = [a * x for x in du]
    pm2, pm1, p0, p1 = (df[k] + au[k] for k in range(4))
    mm1, m0, m1, m2 = (df[k] - au[k] for k in range(1, 5))
    cp = correction(pm2, pm1, p0, p1)
    cm = correction(m2, m1, m0, mm1)
    return 6.0 * fsum + ((pm1 - m1) - (au[2] + au[2]) + (cp - cm))


def primitives(u):
    rinv = 1.0 / u[0]
    kin = 0.5 * (u[1] * u[1] + u[2] * u[2] + u[3] * u[3]) * rinv
    p = (HEAT_RATIO - 1.0) * (u[4] - kin)
    cs = jnp.sqrt(HEAT_RATIO * p * rinv)
    return rinv, p, cs


def fluxes(u, vel, p, normal):
    f = [u[normal], u[1] * vel, u[2] * vel, u[3] * vel, (u[4] + p) * vel]
    f[normal] = f[normal] + p
    return f


def rk_kernel(cfg, *refs):
    r0, r1, q0, q1, rows_all, nblk, lt, has_alias = cfg
    state, lo, hi, left, right, start = refs[:6]
    out = refs[7] if has_alias else refs[6]
    U, FX, SX, RI, PR, CS, DR, SR, RF, CX, EX, sems = refs[8 if has_alias else 7:]
    nq = q1 - q0
    nr = r1 - r0
    st = nblk * SB
    i = pl.program_id(0)
    lane = lax.broadcasted_iota(jnp.int32, (lt, SB, 128), 2)
    lane1 = lax.broadcasted_iota(jnp.int32, (SB, 128), 1)
    sub = lax.broadcasted_iota(jnp.int32, (lt, SB, 128), 1)

    def axial_faces(c, q, base):
        def ld(ref, k, *ix):
            return ref[(*ix, q, slice(None), pl.ds(base + k, SB), slice(None))]

        uu = [ld(U, k, c) for k in range(-2, 4)]
        ff = [ld(U, k, 3) for k in range(-2, 4)] if c == 0 else [ld(FX, k, c - 1) for k in range(-2, 4)]
        a = jnp.maximum(ld(SX, 0), ld(SX, 1))
        df = [ff[k + 1] - ff[k] for k in range(5)]
        du = [uu[k + 1] - uu[k] for k in range(5)]
        return face_flux12(df, du, a, ff[2] + ff[3])

    @pl.when(i == 0)
    def _():
        copies = []
        for l in range(lt):
            ls = pl.ds(128 * l, 128)
            copies.append(pltpu.make_async_copy(
                state.at[:, pl.ds(q0, nq), :, ls], U.at[:, :, l, pl.ds(SB, st), :], sems.at[3 * l]))
            copies.append(pltpu.make_async_copy(
                lo.at[:, pl.ds(q0, nq), :, ls], U.at[:, :, l, pl.ds(0, SB), :], sems.at[3 * l + 1]))
            copies.append(pltpu.make_async_copy(
                hi.at[:, pl.ds(q0, nq), :, ls], U.at[:, :, l, pl.ds(SB + st, SB), :], sems.at[3 * l + 2]))
        for cp in copies:
            cp.start()
        for cp in copies:
            cp.wait()

        def close_end(at_end, to, end, edge):
            @pl.when(at_end)
            def _():
                def close_row(q, _):
                    for c in range(5):
                        cell = U[c, q, :, pl.ds(end, SB), :][:, edge:edge + 1]
                        U[c, q, :, pl.ds(to, SB), :] = jnp.broadcast_to(cell, (lt, SB, 128))
                    return 0

                lax.fori_loop(0, nq, close_row, 0)

        line = lax.axis_index("ax")
        close_end(line == 0, 0, SB, 0)
        close_end(line == lax.axis_size("ax") - 1, SB + st, st, SB - 1)

        def prim_row(q, _):
            def prim_block(b, _):
                ds = pl.ds(pl.multiple_of(b * SB, SB), SB)
                u = [U[c, q, :, ds, :] for c in range(5)]
                rinv, p, cs = primitives(u)
                vel = u[3] * rinv
                f = fluxes(u, vel, p, 3)
                for c in range(1, 5):
                    FX[c - 1, q, :, ds, :] = f[c]
                SX[q, :, ds, :] = jnp.abs(vel) + cs
                RI[q, :, ds, :] = rinv
                PR[q, :, ds, :] = p
                CS[q, :, ds, :] = cs
                return 0

            return lax.fori_loop(0, nblk + 2, prim_block, 0)

        lax.fori_loop(0, nq, prim_row, 0)

        def first_faces(r, _):
            for c in range(5):
                f = axial_faces(c, r + (r0 - q0), SB - 4)
                CX[c, r] = pltpu.roll(f, 4, 1)
            return 0

        lax.fori_loop(0, nr, first_faces, 0)

    base = pl.multiple_of(i * SB + SB, SB)
    ds = pl.ds(base, SB)

    hs = pl.ds(pl.multiple_of(i * SB, SB), SB)
    u = [left[c, hs, :] for c in range(5)]
    rinv, p, cs = primitives(u)
    vel = u[2] * rinv
    f = fluxes(u, vel, p, 2)
    s = jnp.abs(vel) + cs
    a = jnp.maximum(s, pltpu.roll(s, 127, 1))
    for c in range(5):
        df0 = pltpu.roll(f[c], 127, 1) - f[c]
        du0 = pltpu.roll(u[c], 127, 1) - u[c]
        df = [df0 if k == 0 else pltpu.roll(df0, (-k) % 128, 1) for k in range(-2, 3)]
        du = [du0 if k == 0 else pltpu.roll(du0, (-k) % 128, 1) for k in range(-2, 3)]
        EX[c] = face_flux12(df, du, a, f[c] + pltpu.roll(f[c], 127, 1))

    def radial_flux(q):
        u = [U[c, q, :, ds, :] for c in range(5)]
        vel = u[1] * RI[q, :, ds, :]
        f = fluxes(u, vel, PR[q, :, ds, :], 1)
        return u, f, jnp.abs(vel) + CS[q, :, ds, :]

    ne = nr + 5

    def radial_edge(e, carry):
        u, f = carry[:5], carry[5:10]
        q = jnp.clip(e + (r0 - 3) + 1, 0, rows_all - 1) - q0
        un, fn, sn = radial_flux(q)
        for c in range(5):
            DR[c, 0, e] = fn[c] - f[c]
            DR[c, 1, e] = un[c] - u[c]
            RF[c, e] = fn[c] + f[c]
        SR[e] = jnp.maximum(carry[10], sn)
        return (*un, *fn, sn)

    u, f, s = radial_flux(max(r0 - 3, 0) - q0)
    lax.fori_loop(0, ne, radial_edge, (*u, *f, s))

    def radial_face(c, e):
        df = [DR[c, 0, e + k] for k in range(-2, 3)]
        du = [DR[c, 1, e + k] for k in range(-2, 3)]
        return face_flux12(df, du, SR[e], RF[c, e])

    gain = SECTION_GAIN * TIME_STEP

    def one_row(r, low_faces):
        q = r + (r0 - q0)
        row = (r + r0).astype(jnp.float32)
        radius = INNER_RADIUS + RADIAL_STEP * (row + 0.5)
        rr = 1.0 / jnp.full((1, 1, 128), radius, jnp.float32)
        k_low = (gain / 12.0 / RADIAL_STEP) * (INNER_RADIUS + RADIAL_STEP * row) * rr
        k_up = (gain / 12.0 / RADIAL_STEP) * (INNER_RADIUS + RADIAL_STEP * (row + 1.0)) * rr
        k_cycle = (gain / 12.0 * NA / (2.0 * math.pi)) * rr
        k_line = gain / 12.0 / AXIAL_STEP
        k_src = gain * rr
        lr = r + r0
        uc = []
        for c in range(5):
            halo = jnp.where(
                lane1 < 64,
                pltpu.roll(right[c, hs, :], 125 - 8 * lr, 1),
                pltpu.roll(left[c, hs, :], 125 - 8 * lr, 1),
            )
            uc.append(jnp.concatenate([U[c, q, :, ds, :], halo[None]], axis=0))
        hr, hp, hc = primitives([x[lt:] for x in uc])
        rinv = jnp.concatenate([RI[q, :, ds, :], hr], axis=0)
        p = jnp.concatenate([PR[q, :, ds, :], hp], axis=0)
        cs = jnp.concatenate([CS[q, :, ds, :], hc], axis=0)
        vel = uc[2] * rinv
        fc = fluxes(uc, vel, p, 2)
        s = jnp.abs(vel) + cs

        def sh(x, k):
            if k == 0:
                return x[:lt]
            y = pltpu.roll(x, (-k) % 128, 2)
            if k > 0:
                return jnp.where(lane >= 128 - k, y[1:], y[:lt])
            prev = jnp.concatenate([y[lt:], y[:lt - 1]], axis=0) if lt > 1 else y[lt:]
            return jnp.where(lane < -k, prev, y[:lt])

        a_cycle = jnp.maximum(s[:lt], sh(s, 1))
        v0 = vel[:lt]
        src = {
            1: k_src * (uc[2][:lt] * v0 + p[:lt]),
            2: -k_src * (uc[1][:lt] * v0),
        }
        ups = []
        for c in range(5):
            up = radial_face(c, r + 3)
            ups.append(up)
            delta = k_low * low_faces[c] - k_up * up
            ff = [sh(fc[c], k) for k in range(-2, 4)]
            uu = [sh(uc[c], k) for k in range(-2, 4)]
            df = [ff[k + 1] - ff[k] for k in range(5)]
            du = [uu[k + 1] - uu[k] for k in range(5)]
            fa = face_flux12(df, du, a_cycle, ff[2] + ff[3])
            fa1 = pltpu.roll(fa, 1, 2)
            ex = pltpu.roll(EX[c], 126 - 8 * lr, 1)[None]
            prev = jnp.concatenate([ex, fa1[:lt - 1]], axis=0) if lt > 1 else ex
            delta = delta - k_cycle * (fa - jnp.where(lane == 0, prev, fa1))
            fx = axial_faces(c, q, base)
            before = jnp.where(sub == 0, pltpu.roll(CX[c, r], 1, 1), pltpu.roll(fx, 1, 1))
            CX[c, r] = fx
            delta = delta - k_line * (fx - before)
            if c in src:
                delta = delta + src[c]
            delta = delta + SECTION_GAIN * uc[c][:lt]
            for l in range(lt):
                ls = slice(128 * l, 128 * l + 128)
                out[c, r, :, ls] = SECTION_KEEP * start[c, r, :, ls] + delta[l]
        return tuple(ups)

    lax.fori_loop(0, nr, one_row, tuple(radial_face(c, 2) for c in range(5)))


def rk_rows(state, lo, hi, left, right, start, r0, r1, share=None, into=None):
    _, rows, stations, cells = state.shape
    lt = cells // 128
    nblk = stations // SB
    q0, q1 = max(r0 - 3, 0), min(r1 + 3, rows)
    nq, nr = q1 - q0, r1 - r0
    whole = into is not None
    cfg = (r0, r1, q0, q1, rows, nblk, lt, whole and into is not False)
    any_spec = pl.BlockSpec(memory_space=pl.ANY)
    halo_spec = pl.BlockSpec((5, stations, 128), lambda i: (0, 0, 0))
    step = r0 // nr
    in_specs = [any_spec, any_spec, any_spec, halo_spec, halo_spec,
                pl.BlockSpec((5, nr, SB, cells), lambda i: (0, step, i, 0))]
    args = [state, lo, hi, left, right, start]
    alias = {}
    if cfg[-1]:
        in_specs.append(any_spec)
        args.append(into)
        alias = {6: 0}
    if whole:
        out_shape = (5, rows, stations, cells)
        out_spec = pl.BlockSpec((5, nr, SB, cells), lambda i: (0, step, i, 0))
    else:
        group = share // SB
        out_shape = (stations // share, 5, nr, share, cells)
        out_spec = pl.BlockSpec(
            (None, 5, nr, SB, cells), lambda i: (i // group, 0, 0, i % group, 0))
    sp = stations + 2 * SB
    f32 = jnp.float32
    field = pltpu.VMEM((nq, lt, sp, 128), f32)
    return pl.pallas_call(
        functools.partial(rk_kernel, cfg),
        out_shape=jax.ShapeDtypeStruct(out_shape, f32),
        grid=(nblk,),
        in_specs=in_specs,
        out_specs=out_spec,
        scratch_shapes=[
            pltpu.VMEM((5, nq, lt, sp, 128), f32),
            pltpu.VMEM((4, nq, lt, sp, 128), f32),
            field, field, field, field,
            pltpu.VMEM((5, 2, nr + 5, lt, SB, 128), f32),
            pltpu.VMEM((nr + 5, lt, SB, 128), f32),
            pltpu.VMEM((5, nr + 5, lt, SB, 128), f32),
            pltpu.VMEM((5, nr, lt, SB, 128), f32),
            pltpu.VMEM((5, SB, 128), f32),
            pltpu.SemaphoreType.DMA((3 * lt,)),
        ],
        input_output_aliases=alias,
        compiler_params=pltpu.CompilerParams(
            dimension_semantics=("arbitrary",), vmem_limit_bytes=56 << 20),
        name="rk_rows_%d_%d" % (r0, r1),
    )(*args)


def merge_kernel(near, smooth, rows_ref, whole, out):
    for j in range(NF):
        keep = j < rows_ref[...]
        for c in range(5):
            out[c, j] = jnp.where(keep, smooth[c, j], near[c, j])


def merge_near(near, smooth, near_rows, whole):
    groups, _, _, share, cells = near.shape
    spec = pl.BlockSpec((None, 5, NF, share, cells), lambda i: (i, 0, 0, 0, 0))
    return pl.pallas_call(
        merge_kernel,
        out_shape=jax.ShapeDtypeStruct(whole.shape, jnp.float32),
        grid=(groups,),
        in_specs=[spec, spec, pl.BlockSpec((share, 1), lambda i: (i, 0)),
                  pl.BlockSpec(memory_space=pl.ANY)],
        out_specs=pl.BlockSpec((5, NF, share, cells), lambda i: (0, 0, i, 0)),
        input_output_aliases={3: 0},
        name="merge_near",
    )(near, smooth, near_rows[:, None], whole)


def edge_kernel(head, tail, out):
    rows = head.shape[1]
    lane = lax.broadcasted_iota(jnp.int32, head.shape[2:], 1)
    for c in range(5):
        acc = jnp.zeros(head.shape[2:], jnp.float32)
        for r in range(rows):
            ends = jnp.where(lane < 64, head[c, r], tail[c, r])
            ends = pltpu.roll(ends, (8 * r + 3) % 128, 1)
            acc = jnp.where((lane >= 8 * r) & (lane < 8 * r + 8), ends, acc)
        out[c] = acc


def azimuthal_edges(state):
    _, rows, stations, cells = state.shape
    sb = 32
    far = cells // 128 - 1
    return pl.pallas_call(
        edge_kernel,
        out_shape=jax.ShapeDtypeStruct((5, stations, rows * 8), jnp.float32),
        grid=(stations // sb,),
        in_specs=[pl.BlockSpec((5, rows, sb, 128), lambda i: (0, 0, i, 0)),
                  pl.BlockSpec((5, rows, sb, 128), lambda i: (0, 0, i, far))],
        out_specs=pl.BlockSpec((5, sb, rows * 8), lambda i: (0, i, 0)),
        name="azimuthal_edges",
    )(state, state)


def mode_tables():
    n = np.arange(NA // 2)[:, None]
    tables = []
    for parity in (0, 1):
        k = np.arange(parity, NA // 4, 2)[None, :]
        angle = 2.0 * math.pi / NA * ((n * k) % NA)
        tables.append(np.concatenate([np.cos(angle), np.sin(angle)], axis=1).astype(np.float32))
    return tables


def low_pass(cycles, cutoffs):
    half = NA // 2
    pieces, shape = cycles.shape[0], cycles.shape[1:]
    x = jnp.transpose(cycles, (1, 2, 3, 0, 4)).reshape(-1, NA)
    parts = (x[:, :half] + x[:, half:], x[:, :half] - x[:, half:])
    back = []
    for parity, table in enumerate(mode_tables()):
        k = np.arange(parity, NA // 4, 2)
        weight = np.where(k == 0, 1.0 / NA, 2.0 / NA).astype(np.float32)
        k2 = jnp.asarray(np.concatenate([k, k]).astype(np.int32))
        w2 = jnp.asarray(np.concatenate([weight, weight]))
        basis = jnp.asarray(table)
        coef = jnp.einsum("rn,nc->rc", parts[parity], basis, precision=lax.Precision.HIGH)
        gains = jnp.where(k2 < cutoffs[..., None], w2, 0.0)
        coef = (coef.reshape(shape[:3] + (-1,)) * gains[None]).reshape(x.shape[0], -1)
        back.append(jnp.einsum("rc,nc->rn", coef, basis, precision=lax.Precision.HIGH))
    y = jnp.concatenate([back[0] + back[1], back[0] - back[1]], axis=1)
    return jnp.transpose(y.reshape(shape[:3] + (pieces, -1)), (3, 0, 1, 2, 4))


def pressure_of(conserved):
    density = conserved[0]
    kinetic = (
        0.5
        * (conserved[1] * conserved[1] + conserved[2] * conserved[2] + conserved[3] * conserved[3])
        / density
    )
    return (HEAT_RATIO - 1.0) * (conserved[4] - kinetic)


def per_device(step_start, section_state, near_rows, cutoff, gore_map):
    _, rows, stations, cells = section_state.shape
    na, nx = lax.axis_size("az"), lax.axis_size("ax")
    cycle_index, line_index = lax.axis_index("az"), lax.axis_index("ax")
    up_a = [(i, (i + 1) % na) for i in range(na)]
    down_a = [((i + 1) % na, i) for i in range(na)]
    up_x = [(i, (i + 1) % nx) for i in range(nx)]
    down_x = [((i + 1) % nx, i) for i in range(nx)]

    edges = azimuthal_edges(section_state)
    from_left = lax.ppermute(edges, "az", up_a)
    right = lax.ppermute(edges, "az", down_a)
    lanes = jnp.arange(rows * 8, dtype=jnp.int32) % 8
    left = jnp.where(lanes < 3, from_left, edges)

    lo = lax.ppermute(section_state[:, :, -3:], "ax", up_x)
    hi = lax.ppermute(section_state[:, :, :3], "ax", down_x)
    lo = jnp.pad(lo, ((0, 0), (0, 0), (SB - 3, 0), (0, 0)), constant_values=1.0)
    hi = jnp.pad(hi, ((0, 0), (0, 0), (0, SB - 3), (0, 0)), constant_values=1.0)

    rest = functools.partial(rk_rows, section_state, lo, hi, left, right, step_start)
    share = stations // na
    canopy = rows // 2
    jump = pressure_of(section_state[:, canopy - 1]) - pressure_of(section_state[:, canopy + 1])
    total = stations * nx
    station = line_index * stations + jnp.arange(stations, dtype=jnp.int32)
    ramp = 1.0 + 2.0 * station.astype(jnp.float32) / total
    weighted = jump * ramp[:, None] * (1.0 / math.sqrt(total * NA / GORES))
    gores = jnp.arange(GORES, dtype=jnp.int32)
    partial = jnp.sum(
        jnp.where(gore_map[None] == gores[:, None, None], weighted[None], 0.0), axis=(1, 2))
    parts = jnp.broadcast_to(jnp.pad(partial, (0, 128 - GORES)), (na * nx, 128))
    parts = lax.all_to_all(parts, ("az", "ax"), 0, 0, tiled=True)
    near = rest(0, NF, share=share)
    parts, near = lax.optimization_barrier((parts, near))
    spread = lax.all_to_all(near, "az", 0, 0, tiled=True)
    whole = rest(NF, 2 * NF, into=False)
    spread, whole = lax.optimization_barrier((spread, whole))
    cutoffs = lax.dynamic_slice_in_dim(cutoff, cycle_index * share, share, axis=1)
    kept = low_pass(spread, cutoffs)
    kept, whole = lax.optimization_barrier((kept, whole))
    smooth = lax.all_to_all(kept, "az", 0, 0, tiled=True)
    whole = rest(2 * NF, rows, into=whole)

    gore_loads = jnp.sum(parts, axis=0)[:GORES]
    new_state = merge_near(near, smooth, near_rows, whole)
    return (new_state, gore_loads)


def solution(mesh):
    in_specs = (
        P(None, None, "ax", "az"),
        P(None, None, "ax", "az"),
        P("ax"),
        P(None, "ax"),
        P("ax", "az"),
    )
    out_specs = (P(None, None, "ax", "az"), P())
    return jax.shard_map(
        per_device, mesh=mesh, in_specs=in_specs, out_specs=out_specs, check_vma=False
    )
```
